512 devices in a mesh: dp: 16 (over x, y_lo), expert: 16 (over z, y_hi), tensor: 2 (over core).
Axes of the slice: x: 4, y: 8 (y_hi: 2, y_lo: 4; y = y_hi * 4 + y_lo), z: 8, core: 2. Of those that a mesh axis runs over, the one named last changes fastest.
Arguments:
- tokens: bfloat16 [32768, 2048], P(('dp', 'expert'), 'tensor'), may hold values from -24 to 24
- routes: int32 [32768, 4], P(('dp', 'expert')), may hold values from 0 to 15, all different within a row; in each aligned block of 128 rows (0 to 127, 128 to 255, ...) at most 40 rows name the same one
- gates: float32 [32768, 4], P(('dp', 'expert')), may hold values from 0.05 to 1
- w_in: bfloat16 [16, 768, 2048], P('expert', 'tensor'), may hold values from -0.125 to 0.125
- w_out: bfloat16 [16, 768, 2048], P('expert', 'tensor'), may hold values from -0.21875 to 0.21875
- cotangent: bfloat16 [32768, 2048], P(('dp', 'expert'), 'tensor'), may hold values from -8 to 8
Outputs:
- mixed: bfloat16 [32768, 2048], P(('dp', 'expert'), 'tensor')
- grad_tokens: bfloat16 [32768, 2048], P(('dp', 'expert'), 'tensor')
- grad_gates: float32 [32768, 4], P(('dp', 'expert'))
- grad_in: float32 [16, 768, 2048], P('expert', 'tensor', 'dp')
- grad_out: float32 [16, 768, 2048], P('expert', 'tensor', 'dp')
The draws below stay inside these ranges and needn't reach their ends.
Inputs may be any that keep to these rules, and one draw needn't show every extreme that they name: `routes`: each row names 4 different experts. The rows of one device (aligned blocks of 128 rows) name no expert more than 40 times, and in every draw some block names some expert exactly 40 times.
All inputs are finite; a program needn't handle non-finite values.
Results may differ from the reference program's by a relative error of at most 0.018.
Values may be sent and summed in bfloat16 or wider, within the bound.
A program may use at most 64 MiB of HBM per device.

```python
import math
import jax
import jax.numpy as jnp
import numpy as np
from jax import lax

D = 2048
F = 768
TOPK = 4
TOK_DEV = 128
EXPERTS = 16
TOKENS = 32768
CAP = 40
N_DP = 16
N_EXPERT = 16


def strengthened(result, stream_key, source, target, shards_of, factor):
    owner, partner = [(jnp.arange(result.shape[axis_at]) // (result.shape[axis_at] // shards_of)).reshape([-1 if axis == axis_at else 1 for axis in range(result.ndim)]) for axis_at in (source, target)]
    chosen = jax.random.permutation(stream_key, shards_of)[partner]
    strong = (owner == chosen) | (owner == (partner + shards_of // 2) % shards_of)
    return jnp.where(strong, factor * result, result)


def block_scale(stream_key, shape, pieces, low, largest):
    def one(position, shards_of):
        draws = jax.random.uniform(jax.random.fold_in(jax.random.fold_in(stream_key, 6), position), (shards_of,), jnp.float32, low / len(pieces), largest / len(pieces))
        return jnp.repeat(jnp.exp(draws), shape[position] // shards_of).reshape((-1,) + (1,) * (len(shape) - position - 1))

    gain = one(*pieces[0])
    for cut in pieces[1:]:
        gain = gain * one(*cut)
    return gain


def shared_out(rng, own, number, rows, number_of, top, bound, skew):
    ranking = jax.random.permutation(rng, number_of)
    packed, common = portions_of(number_of, rows * top, bound, skew, True), portions_of(number_of, rows * top, bound, skew, False)
    places = jnp.arange(number_of)

    def named(tallies, turn):
        used = int((tallies > 0).sum())
        fixed = max(1, used // 4)
        passed = fixed + (places - fixed + turn * (used - fixed)) % max(1, number_of - fixed)
        return jnp.zeros((number_of,), jnp.int32).at[ranking[jnp.where(places < fixed, places, passed)]].set(jnp.asarray(tallies, jnp.int32))

    tallies = jnp.where(number % 4 == 0, named(packed, number // 4), named(common, number - number // 4 - 1))
    mixed = jax.random.permutation(jax.random.fold_in(own, 3), number_of)
    donor, sink = mixed[0:number_of // 2 * 2:2], mixed[1:number_of // 2 * 2:2]
    slack = jnp.minimum(tallies[donor] - 1, bound - tallies[sink]) // 2
    slack = jnp.where((donor == ranking[0]) | (sink == ranking[0]) | (tallies[sink] == 0), 0, jnp.maximum(slack, 0))
    passed = jax.random.randint(jax.random.fold_in(own, 4), (number_of // 2,), 0, 1 << 20) % (slack + 1)
    tallies = tallies.at[donor].add(-passed).at[sink].add(passed)
    items = jnp.searchsorted(jnp.cumsum(tallies), jnp.arange(rows * top), side="right").astype(jnp.int32)
    grid = items.reshape(top, rows).T
    grid = grid[jax.random.permutation(jax.random.fold_in(own, 1), rows)]
    turn = jax.random.randint(jax.random.fold_in(own, 2), (rows, 1), 0, top)
    return jnp.take_along_axis(grid, (jnp.arange(top)[None, :] + turn) % top, axis=1)


def portions_of(number_of, total, limit, slope, full):
    weights = [(1 << 20) // math.isqrt(standing ** slope) + 1 for standing in range(1, number_of + 1)]
    largest = limit if full else min(limit, max(-(-total // number_of), total * weights[0] // sum(weights)))
    least = 1 if total - largest >= number_of - 1 else 0
    given, surplus = [largest] + [least] * (number_of - 1), total - largest - least * (number_of - 1)
    while surplus > 0:
        movable = [i for i in range(1, number_of) if given[i] < largest] or [i for i in range(1, number_of) if given[i] < limit]
        mass, left = sum([weights[i] for i in movable]), surplus
        for i in movable:
            extra = min(limit - given[i], max(1, left * weights[i] // mass), surplus)
            given[i] = given[i] + extra
            surplus = surplus - extra
    return np.array(given)


def normal_values(stream_key, shape, width, reach, cuts=(), kind=jnp.bfloat16):
    result = width * jax.random.normal(stream_key, shape, jnp.float32)
    if cuts:
        result = result * block_scale(stream_key, shape, cuts, -0.22, 0.18)
    return jnp.clip(result, -reach, reach).astype(kind)


def noise_with(rng, shape, deviation, most, pieces, heavy, kind=jnp.bfloat16):
    entries = deviation * jax.random.normal(rng, shape, jnp.float32)
    if pieces:
        entries = entries * block_scale(rng, shape, pieces, -0.22, 0.18)
    return jnp.clip(strengthened(entries, jax.random.fold_in(rng, 3), *heavy), -most, most).astype(kind)


def setup_inputs(seed: int = 0) -> dict:
    key_list = jax.random.split(jax.random.key(seed), 7)
    tokens = noise_with(key_list[0], (TOKENS, D), 1.0, 24.0, ((0, 256), (1, 2)), (0, 1, 256, 6.0))
    routes_keys = jax.random.split(jax.random.fold_in(key_list[1], 1), TOKENS // TOK_DEV)
    routes_turns = jax.random.permutation(jax.random.fold_in(key_list[1], 3), TOKENS // TOK_DEV)
    routes = jax.vmap(lambda own, number: shared_out(jax.random.fold_in(key_list[1], 2), own, number, TOK_DEV, EXPERTS, TOPK, CAP, 2))(routes_keys, routes_turns).reshape((TOKENS, TOPK))
    gates = jnp.clip(jnp.exp(math.log(1.0) - 2.9957323 * jax.random.uniform(key_list[2], (TOKENS, TOPK), jnp.float32) ** block_scale(key_list[2], (TOKENS, TOPK), ((0, 256),), -0.2, 0.2)), 0.05, 1.0)
    w_in = normal_values(key_list[3], (EXPERTS, F, D), D ** -0.5, 0.125, ((0, 16), (1, 2)))
    w_out = normal_values(key_list[4], (EXPERTS, F, D), F ** -0.5, 0.21875, ((0, 16), (1, 2)))
    cotangent = noise_with(key_list[5], (TOKENS, D), 0.3, 8.0, ((0, 256), (1, 2)), (0, 1, 256, 6.0))
    return {"tokens": tokens, "routes": routes, "gates": gates, "w_in": w_in, "w_out": w_out, "cotangent": cotangent}


def silu_slope(pre_value):
    logistic = jax.nn.sigmoid(pre_value)
    return logistic * (1.0 + pre_value * (1.0 - logistic))


def take_rows(table, index):
    return jax.vmap(lambda rows_table, row_index: rows_table[row_index])(table, index)


def reference(tokens, routes, gates, w_in, w_out, cotangent):
    blocks = N_DP * N_EXPERT
    pair_count = TOK_DEV * TOPK
    block_routes = routes.reshape(blocks, pair_count)
    one_hot = (block_routes[:, :, None] == jnp.arange(EXPERTS, dtype=jnp.int32)[None, None, :]).astype(jnp.int32)
    rank_before = jnp.cumsum(one_hot, axis=1) - one_hot
    slot_index = jnp.sum(rank_before * one_hot, axis=2).astype(jnp.int32)
    destination = (block_routes * CAP + slot_index).astype(jnp.int32)
    block_ids = jnp.broadcast_to(jnp.arange(blocks, dtype=jnp.int32)[:, None], (blocks, pair_count))
    pair_ids = jnp.broadcast_to(jnp.arange(pair_count, dtype=jnp.int32)[None, :], (blocks, pair_count))
    source = jnp.full((blocks, EXPERTS * CAP), pair_count, jnp.int32).at[block_ids, destination].set(pair_ids)
    source = source.reshape(blocks, EXPERTS, CAP).transpose(1, 0, 2)
    zero_rows = jnp.zeros((blocks, 1, D), tokens.dtype)
    tokens_pad = jnp.concatenate([tokens.reshape(blocks, TOK_DEV, D), zero_rows], axis=1)
    cotangent_pad = jnp.concatenate([cotangent.reshape(blocks, TOK_DEV, D), zero_rows], axis=1)
    gates_pad = jnp.concatenate([gates.reshape(blocks, pair_count), jnp.zeros((blocks, 1), jnp.float32)], axis=1)
    cotangent_wide = cotangent.reshape(blocks, TOK_DEV, D).astype(jnp.float32)
    slot_tok = slot_index.reshape(blocks, TOK_DEV, TOPK)
    gates_tok = gates.reshape(blocks, TOK_DEV, TOPK)

    def expert_step(carry, inputs):
        mixed_acc, tok_acc, gate_acc = carry
        expert_id, source_e, w_in_e, w_out_e = inputs
        source_row = (source_e // TOPK).astype(jnp.int32)
        rows = take_rows(tokens_pad, source_row).reshape(blocks * CAP, D)
        pre_value = jnp.dot(rows, w_in_e.T, preferred_element_type=jnp.float32)
        hidden = jax.nn.silu(pre_value).astype(jnp.bfloat16)
        expert_out = jnp.dot(hidden, w_out_e, preferred_element_type=jnp.float32).astype(jnp.bfloat16)
        gate_slots = take_rows(gates_pad, source_e).reshape(blocks * CAP, 1)
        cot_rows = take_rows(cotangent_pad, source_row).reshape(blocks * CAP, D)
        scaled = (gate_slots * cot_rows.astype(jnp.float32)).astype(jnp.bfloat16)
        grad_hidden = jnp.dot(scaled, w_out_e.T, preferred_element_type=jnp.float32)
        grad_pre = (grad_hidden * silu_slope(pre_value)).astype(jnp.bfloat16)
        grad_rows = jnp.dot(grad_pre, w_in_e, preferred_element_type=jnp.float32).astype(jnp.bfloat16)
        group_rows = rows.reshape(N_DP, N_EXPERT * CAP, D).astype(jnp.float32)
        group_pre = grad_pre.reshape(N_DP, N_EXPERT * CAP, F).astype(jnp.float32)
        group_hidden = hidden.reshape(N_DP, N_EXPERT * CAP, F).astype(jnp.float32)
        group_scaled = scaled.reshape(N_DP, N_EXPERT * CAP, D).astype(jnp.float32)
        in_part = jnp.einsum("grf,grd->gfd", group_pre, group_rows).astype(jnp.bfloat16)
        grad_in_e = jnp.sum(in_part.astype(jnp.float32), axis=0)
        out_part = jnp.einsum("grf,grd->gfd", group_hidden, group_scaled).astype(jnp.bfloat16)
        grad_out_e = jnp.sum(out_part.astype(jnp.float32), axis=0)
        hits = (block_routes == expert_id).reshape(blocks, TOK_DEV, TOPK)
        hit_wide = hits.astype(jnp.float32)
        tok_slot = jnp.sum(slot_tok * hits.astype(jnp.int32), axis=2).astype(jnp.int32)
        tok_gate = jnp.sum(gates_tok * hit_wide, axis=2)
        tok_mask = jnp.sum(hit_wide, axis=2)
        out_tok = take_rows(expert_out.reshape(blocks, CAP, D), tok_slot).astype(jnp.float32)
        mixed_acc = mixed_acc + tok_gate[:, :, None] * out_tok
        inner = jnp.sum(cotangent_wide * out_tok, axis=2)
        gate_acc = gate_acc + inner[:, :, None] * hit_wide
        back_tok = take_rows(grad_rows.reshape(blocks, CAP, D), tok_slot).astype(jnp.float32)
        tok_acc = tok_acc + tok_mask[:, :, None] * back_tok
        return (mixed_acc, tok_acc, gate_acc), (grad_in_e, grad_out_e)

    start_carry = (jnp.zeros((blocks, TOK_DEV, D), jnp.float32), jnp.zeros((blocks, TOK_DEV, D), jnp.float32), jnp.zeros((blocks, TOK_DEV, TOPK), jnp.float32))
    inputs = (jnp.arange(EXPERTS, dtype=jnp.int32), source, w_in, w_out)
    (mixed_acc, tok_acc, gate_acc), (grad_in, grad_out) = lax.scan(expert_step, start_carry, inputs)
    mixed = mixed_acc.reshape(TOKENS, D).astype(jnp.bfloat16)
    grad_tokens = tok_acc.reshape(TOKENS, D).astype(jnp.bfloat16)
    grad_gates = gate_acc.reshape(TOKENS, TOPK)
    return (mixed, grad_tokens, grad_gates, grad_in, grad_out)
```

```python
import functools

import jax
import jax.numpy as jnp
from jax import lax
from jax.experimental import pallas as pl
from jax.experimental.pallas import tpu as pltpu
from jax.sharding import PartitionSpec as P

MESH = pl.DeviceIdType.MESH
F32, BF16 = jnp.float32, jnp.bfloat16

NX, NYL = 4, 4
NZ, NYH = 8, 2
TOK = 128
CAP = 40
HEAD = 32
SLOTS = 2 * CAP
ROWS = NZ * SLOTS
HALF = 1024
HID = 384
CHUNKS = 4

PH_TOK_HEAD, PH_TOK_REST, PH_SCALED, PH_OUT, PH_BACK = 0, 1, 2, 3, 4
PHASES = PH_BACK + CHUNKS
SB_WIN, SB_WOUT, SB_ROWS, SB_HID, SB_SCALED, SB_PRE, SB_GATE = range(7)
YP_ROUTES, YP_GATES, YP_TOK, YP_COT, YP_MIX, YP_GG, YP_BACK = range(7)


def dot(a, b, dims):
    return lax.dot_general(a, b, (dims, ((), ())), preferred_element_type=F32)


NN = ((1,), (0,))
NT = ((1,), (1,))


def kernel(
    tok_ref, cot_ref, rt_ref, gt_ref, win_ref, wout_ref,
    mix_ref, gtok_ref, gg_ref, gin_ref, gout_ref,
    tok2, cot2, rt2, gt2, sel, rankm, gatem,
    send_tok, send_sc, rows, scal, hid, pre, slope, wi, wo,
    out, back, rout, rback, g_hi, g_lo, sel_t, hid_t, pre_t,
    mixo, mixs, mixr, bko, bks, bkr, ggp, ggs, ggr, ggm, ggx,
    part, xa, xb, xs, x1, x2, xd1, xd2, xq, xqb, yr,
    zs, zr, ss, sr, ps, pr, xsm, xrm, ys, yrm,
):
    dp = lax.axis_index("dp")
    ex = lax.axis_index("expert")
    c = lax.axis_index("tensor")
    x, yl = dp // NYL, dp % NYL
    z, yh = ex // NYH, ex % NYH
    sib = {"tensor": 1 - c}
    mirror = {"dp": x * NYL + (NYL - 1 - yl), "expert": z * NYH + (1 - yh)}
    x_up = {"dp": ((x + 1) % NX) * NYL + yl}
    x_dn = {"dp": ((x + NX - 1) % NX) * NYL + yl}

    def z_dev(other):
        return {"expert": other * NYH + yh}

    def y_dev(other):
        return {"dp": x * NYL + other}

    def rcopy(src, dst, send, recv, dev):
        return pltpu.make_async_remote_copy(
            src_ref=src, dst_ref=dst, send_sem=send, recv_sem=recv,
            device_id=dev, device_id_type=MESH,
        )

    barrier = pltpu.get_barrier_semaphore()

    def greet(dev):
        pl.semaphore_signal(barrier, inc=1, device_id=dev, device_id_type=MESH)

    for step in range(1, NZ):
        greet(z_dev((z + step) % NZ))
    for step in range(1, NYL):
        greet(y_dev((yl + step) % NYL))
    greet(sib)
    greet(mirror)
    greet(x_up)
    greet(x_dn)

    tok2[0:TOK, :] = tok_ref[...]
    cot2[0:TOK, :] = cot_ref[...]
    rt2[:, 0:TOK] = rt_ref[...]
    gt2[:, 0:TOK] = gt_ref[...]
    before = (
        lax.broadcasted_iota(jnp.int32, (TOK, TOK), 0)
        < lax.broadcasted_iota(jnp.int32, (TOK, TOK), 1)
    ).astype(F32).astype(BF16)
    names = 2 * lax.broadcasted_iota(jnp.int32, (16, TOK), 0) + yh

    def place(block):
        cols = slice(block * TOK, (block + 1) * TOK)
        hits = jnp.zeros((16, TOK), F32)
        gate = jnp.zeros((16, TOK), F32)
        for k in range(4):
            hit = rt2[k : k + 1, cols] == names
            hits = hits + jnp.where(hit, 1.0, 0.0)
            gate = gate + jnp.where(hit, gt2[k : k + 1, cols], 0.0)
        rank = dot(hits.astype(BF16), before, NN)
        rank = jnp.where(hits > 0.0, rank, -5.0)
        for e in range(NZ):
            rankm[e, :, cols] = rank[e : e + 1]
            gatem[e, :, cols] = gate[e : e + 1]

    place(0)
    head_slot = lax.broadcasted_iota(jnp.int32, (HEAD, TOK), 0).astype(F32)

    def own_head(e, carry):
        choose = jnp.where(rankm[e, :, 0:TOK] == head_slot, 1.0, 0.0).astype(BF16)
        at = pl.multiple_of(e * SLOTS, 16)
        send_tok[pl.ds(at, HEAD), :] = dot(choose, tok2[0:TOK, :], NN).astype(BF16)
        return carry

    lax.fori_loop(0, NZ, own_head, 0)

    pl.semaphore_wait(barrier, (NZ - 1) + (NYL - 1) + 4)

    y_in = [
        rcopy(rt_ref, rt2.at[:, pl.ds(TOK, TOK)], ps.at[YP_ROUTES], pr.at[YP_ROUTES], mirror),
        rcopy(gt_ref, gt2.at[:, pl.ds(TOK, TOK)], ps.at[YP_GATES], pr.at[YP_GATES], mirror),
        rcopy(tok_ref, tok2.at[pl.ds(TOK, TOK), :], ps.at[YP_TOK], pr.at[YP_TOK], mirror),
        rcopy(cot_ref, cot2.at[pl.ds(TOK, TOK), :], ps.at[YP_COT], pr.at[YP_COT], mirror),
    ]
    for cp in y_in:
        cp.start()

    def z_copy(src, dst, lo, size, cols, phase, other, sender):
        s_at = pl.multiple_of(other * SLOTS + lo, 16)
        d_at = pl.multiple_of(sender * SLOTS + lo, 16)
        return rcopy(
            src.at[pl.ds(s_at, size), cols], dst.at[pl.ds(d_at, size), cols],
            zs.at[phase, other], zr.at[phase, sender], z_dev(other),
        )

    full = pl.ds(0, HALF)

    def z_send(src, dst, lo, size, cols, phase):
        def one(step, carry):
            z_copy(src, dst, lo, size, cols, phase, (z + step) % NZ, z).start()
            return carry

        lax.fori_loop(1, NZ, one, 0)

    def z_recv(src, dst, lo, size, cols, phase):
        def one(step, carry):
            other = (z + step) % NZ
            z_copy(src, dst, lo, size, cols, phase, other, other).wait_recv()
            return carry

        lax.fori_loop(1, NZ, one, 0)

    def z_sent(src, dst, lo, size, cols, phase):
        def one(step, carry):
            z_copy(src, dst, lo, size, cols, phase, (z + step) % NZ, z).wait_send()
            return carry

        lax.fori_loop(1, NZ, one, 0)

    here = pl.ds(pl.multiple_of(z * SLOTS, 16), SLOTS)
    rows_own, scal_own = rows.at[c], scal.at[c]
    z_send(send_tok, rows_own, 0, HEAD, full, PH_TOK_HEAD)

    w_other = pl.ds(pl.multiple_of((1 - c) * HALF, 128), HALF)
    w_mine = pl.ds(pl.multiple_of(c * HALF, 128), HALF)
    w_cp = [
        rcopy(win_ref.at[:, w_other], wi.at[c], ss.at[SB_WIN], sr.at[SB_WIN], sib),
        rcopy(wout_ref.at[:, w_other], wo.at[c], ss.at[SB_WOUT], sr.at[SB_WOUT], sib),
    ]
    for cp in w_cp:
        cp.start()
    wi[c] = win_ref[:, w_mine]
    wo[c] = wout_ref[:, w_mine]

    r_id = lax.broadcasted_iota(jnp.int32, (SLOTS, 2 * TOK), 0)
    t_id = lax.broadcasted_iota(jnp.int32, (SLOTS, 2 * TOK), 1)
    late = jnp.where(t_id >= TOK, 1, 0)
    second = jnp.where(
        r_id < 2 * HEAD,
        jnp.where(r_id >= HEAD, 1, 0),
        jnp.where(r_id >= HEAD + CAP, 1, 0),
    )
    slot = jnp.where(
        r_id < HEAD, r_id, jnp.where(r_id < HEAD + CAP, r_id - HEAD, r_id - CAP)
    )
    slot_map = jnp.where(second == late, slot, -1).astype(F32)

    y_in[0].wait_recv()
    y_in[1].wait_recv()
    place(1)
    y_in[2].wait_recv()

    def gather_tok(e, carry):
        choose = jnp.where(rankm[e] == slot_map, 1.0, 0.0)
        at = pl.multiple_of(e * SLOTS, 16)
        sel[pl.ds(at, SLOTS), :] = choose
        send_tok[pl.ds(at + HEAD, SLOTS - HEAD), :] = dot(
            choose[HEAD:].astype(BF16), tok2[...], NN
        ).astype(BF16)
        return carry

    lax.fori_loop(0, NZ, gather_tok, 0)
    z_send(send_tok, rows_own, HEAD, SLOTS - HEAD, full, PH_TOK_REST)
    rows[c, here, :] = send_tok[here, :]

    y_in[3].wait_recv()

    def gather_cot(e, carry):
        at = pl.ds(pl.multiple_of(e * SLOTS, 16), SLOTS)
        choose = sel[at, :]
        gate = jnp.sum(choose * gatem[e], axis=1, keepdims=True)
        send_sc[at, :] = (gate * dot(choose.astype(BF16), cot2[...], NN)).astype(BF16)
        return carry

    lax.fori_loop(0, NZ, gather_cot, 0)
    z_send(send_sc, scal_own, 0, SLOTS, full, PH_SCALED)
    scal[c, here, :] = send_sc[here, :]

    def gates_of(e, carry):
        at = pl.ds(pl.multiple_of(e * SLOTS, 16), SLOTS)
        out_gate = sel[at, :] * gatem[e]
        slope[at, 0 : 2 * TOK] = out_gate
        return carry

    lax.fori_loop(0, NZ, gates_of, 0)

    def turn(i, carry):
        at = pl.ds(pl.multiple_of(i * 128, 128), 128)
        g_t = slope[at, 0 : 2 * TOK].T
        hi = g_t.astype(BF16)
        g_hi[:, at] = hi
        g_lo[:, at] = (g_t - hi.astype(F32)).astype(BF16)
        sel_t[:, at] = sel[at, :].T.astype(BF16)
        return carry

    lax.fori_loop(0, ROWS // 128, turn, 0)

    z_recv(send_tok, rows_own, 0, HEAD, full, PH_TOK_HEAD)
    z_recv(send_tok, rows_own, HEAD, SLOTS - HEAD, full, PH_TOK_REST)
    cp_rows = rcopy(rows.at[c], rows.at[c], ss.at[SB_ROWS], sr.at[SB_ROWS], sib)
    cp_rows.start()
    cp_rows.wait_recv()

    TILE = 320

    def tile(i):
        return pl.ds(pl.multiple_of(i * TILE, 64), TILE)

    def forward(i, carry):
        at = tile(i)
        v = dot(rows[0, at, :], win_ref[:, 0:HALF], NT) + dot(
            rows[1, at, :], win_ref[:, HALF:], NT
        )
        s = 1.0 / (1.0 + jnp.exp(-v))
        hid[c, at, :] = (v * s).astype(BF16)
        slope[at, :] = s * (1.0 + v * (1.0 - s))
        return carry

    lax.fori_loop(0, ROWS // TILE, forward, 0)
    cp_hid = rcopy(hid.at[c], hid.at[c], ss.at[SB_HID], sr.at[SB_HID], sib)
    cp_hid.start()
    w_cp[0].wait_recv()
    w_cp[1].wait_recv()
    cp_hid.wait_recv()

    def project(i, carry):
        at = tile(i)
        out[at, :] = (dot(hid[0, at, :], wo[0], NN) + dot(hid[1, at, :], wo[1], NN)).astype(BF16)
        return carry

    lax.fori_loop(0, ROWS // TILE, project, 0)
    z_send(out, rout, 0, SLOTS, full, PH_OUT)
    rout[here, :] = out[here, :]

    z_recv(send_sc, scal_own, 0, SLOTS, full, PH_SCALED)
    cp_sc = rcopy(scal.at[c], scal.at[c], ss.at[SB_SCALED], sr.at[SB_SCALED], sib)
    cp_sc.start()
    cp_sc.wait_recv()

    def backward(i, carry):
        at = tile(i)
        v = dot(scal[0, at, :], wout_ref[:, 0:HALF], NT) + dot(
            scal[1, at, :], wout_ref[:, HALF:], NT
        )
        pre[c, at, :] = (v * slope[at, :]).astype(BF16)
        return carry

    lax.fori_loop(0, ROWS // TILE, backward, 0)
    cp_pre = rcopy(pre.at[c], pre.at[c], ss.at[SB_PRE], sr.at[SB_PRE], sib)
    cp_pre.start()
    cp_pre.wait_recv()

    def project_back(i, carry):
        at = tile(i)
        back[at, :] = (dot(pre[0, at, :], wi[0], NN) + dot(pre[1, at, :], wi[1], NN)).astype(BF16)
        return carry

    lax.fori_loop(0, ROWS // TILE, project_back, 0)
    WIDE = HALF // CHUNKS

    def piece(q):
        return pl.ds(q * WIDE, WIDE)

    for q in range(CHUNKS):
        z_send(back, rback, 0, SLOTS, piece(q), PH_BACK + q)
    rback[here, :] = back[here, :]

    def flip(i, carry):
        at = pl.ds(pl.multiple_of(i * 128, 128), 128)
        hid_t[:, at] = hid[c, at, :].astype(F32).T.astype(BF16)
        pre_t[:, at] = pre[c, at, :].astype(F32).T.astype(BF16)
        return carry

    lax.fori_loop(0, ROWS // 128, flip, 0)
    for h in range(2):
        def weigh(n, carry, h=h):
            src = pl.ds(pl.multiple_of(n * 256, 256), 256)
            dst = pl.ds(pl.multiple_of(h * HALF + n * 256, 256), 256)
            part[0:HID, dst] = dot(pre_t[...], rows[h, :, src], NN).astype(BF16)
            part[HID:, dst] = dot(hid_t[...], scal[h, :, src], NN).astype(BF16)
            return carry

        lax.fori_loop(0, HALF // 256, weigh, 0)

    XW = 512
    XH = XW // 2

    def x_cols(other, half):
        return pl.ds(pl.multiple_of(other * XW + half * XH, 256), XH)

    up, dn, far = (x + 1) % NX, (x + NX - 1) % NX, (x + 2) % NX
    x_first = [
        rcopy(part.at[:, x_cols(far, 0)], xa, xsm.at[0], xrm.at[0], x_up),
        rcopy(part.at[:, x_cols(far, 1)], xb, xsm.at[1], xrm.at[1], x_dn),
        rcopy(part.at[:, x_cols(up, 1)], xd1, xsm.at[2], xrm.at[2], x_up),
        rcopy(part.at[:, x_cols(dn, 0)], xd2, xsm.at[3], xrm.at[3], x_dn),
    ]
    for cp in x_first:
        cp.start()
    x_first[0].wait_recv()
    xs[0] = (part[:, x_cols(up, 0)].astype(F32) + xa[...].astype(F32)).astype(BF16)
    x_first[1].wait_recv()
    xs[1] = (part[:, x_cols(dn, 1)].astype(F32) + xb[...].astype(F32)).astype(BF16)
    x_second = [
        rcopy(xs.at[0], x1, xsm.at[4], xrm.at[4], x_up),
        rcopy(xs.at[1], x2, xsm.at[5], xrm.at[5], x_dn),
    ]
    for cp in x_second:
        cp.start()

    z_recv(out, rout, 0, SLOTS, full, PH_OUT)

    def mix(n, carry):
        at = pl.ds(pl.multiple_of(n * 256, 256), 256)
        m = dot(g_hi[...], rout[:, at], NN) + dot(g_lo[...], rout[:, at], NN)
        mixo[:, at] = m[0:TOK]
        mixs[:, at] = m[TOK:].astype(BF16)
        return carry

    lax.fori_loop(0, HALF // 256, mix, 0)
    cp_mix = rcopy(mixs, mixr, ps.at[YP_MIX], pr.at[YP_MIX], mirror)
    cp_mix.start()

    def inner(e, acc):
        at = pl.ds(pl.multiple_of(e * SLOTS, 16), SLOTS)
        dots = dot(rout[at, :], cot2[...], NT) * sel[at, :]
        per_token = jnp.sum(dots, axis=0, keepdims=True)
        hit = rt2[...] == 2 * e + yh
        return acc + jnp.where(hit, per_token, 0.0)

    gate_part = lax.fori_loop(0, NZ, inner, jnp.zeros((4, 2 * TOK), F32))
    ggp[...] = gate_part[:, 0:TOK]
    ggs[...] = gate_part[:, TOK:]
    cp_gg = rcopy(ggs, ggr, ps.at[YP_GG], pr.at[YP_GG], mirror)
    cp_gg.start()

    x_first[2].wait_recv()
    x_first[3].wait_recv()
    x_second[0].wait_recv()
    x_second[1].wait_recv()
    xq[:, 0:XH] = (
        part[:, x_cols(x, 0)].astype(F32) + x1[...].astype(F32) + xd2[...].astype(F32)
    )
    xq[:, XH:] = (
        part[:, x_cols(x, 1)].astype(F32) + x2[...].astype(F32) + xd1[...].astype(F32)
    )
    xqb[...] = xq[...].astype(BF16)

    def y_cols(other):
        return pl.ds(pl.multiple_of(other * 128, 128), 128)

    def y_copy(other, sender):
        return rcopy(xqb.at[:, y_cols(other)], yr.at[sender], ys.at[other], yrm.at[sender], y_dev(other))

    for step in range(1, NYL):
        y_copy((yl + step) % NYL, yl).start()

    cp_gg.wait_recv()
    ggm[...] = ggp[...] + ggr[...]
    cp_gs = rcopy(ggm, ggx, ss.at[SB_GATE], sr.at[SB_GATE], sib)
    cp_gs.start()
    cp_mix.wait_recv()
    mix_ref[...] = (mixo[...] + mixr[...].astype(F32)).astype(BF16)
    cp_gs.wait_recv()
    gg_ref[...] = ggm[...] + ggx[...]

    total = xq[:, y_cols(yl)]
    for step in range(1, NYL):
        other = (yl + step) % NYL
        y_copy(other, other).wait_recv()
        total = total + yr[other].astype(F32)
    gin_ref[...] = total[0:HID]
    gout_ref[...] = total[HID:]

    cp_back = []
    for q in range(CHUNKS):
        z_recv(back, rback, 0, SLOTS, piece(q), PH_BACK + q)
        b = dot(sel_t[...], rback[:, piece(q)], NN)
        bko[:, piece(q)] = b[0:TOK]
        bks[:, piece(q)] = b[TOK:].astype(BF16)
        cp = rcopy(
            bks.at[:, piece(q)], bkr.at[:, piece(q)],
            ps.at[YP_BACK + q], pr.at[YP_BACK + q], mirror,
        )
        cp.start()
        cp_back.append(cp)
    for q in range(CHUNKS):
        cp_back[q].wait_recv()
        gtok_ref[:, piece(q)] = (bko[:, piece(q)] + bkr[:, piece(q)].astype(F32)).astype(BF16)

    z_sent(send_tok, rows_own, 0, HEAD, full, PH_TOK_HEAD)
    z_sent(send_tok, rows_own, HEAD, SLOTS - HEAD, full, PH_TOK_REST)
    z_sent(send_sc, scal_own, 0, SLOTS, full, PH_SCALED)
    z_sent(out, rout, 0, SLOTS, full, PH_OUT)
    for q in range(CHUNKS):
        z_sent(back, rback, 0, SLOTS, piece(q), PH_BACK + q)
    for step in range(1, NYL):
        y_copy((yl + step) % NYL, yl).wait_send()
    for cp in y_in + w_cp + x_first + x_second + cp_back:
        cp.wait_send()
    for cp in (cp_rows, cp_hid, cp_sc, cp_pre, cp_mix, cp_gg, cp_gs):
        cp.wait_send()


def per_device(tokens, routes, gates, w_in, w_out, cotangent):
    vmem = pl.BlockSpec(memory_space=pltpu.VMEM)
    V = pltpu.VMEM
    dma = pltpu.SemaphoreType.DMA
    outs = pl.pallas_call(
        kernel,
        out_shape=(
            jax.ShapeDtypeStruct((TOK, HALF), BF16),
            jax.ShapeDtypeStruct((TOK, HALF), BF16),
            jax.ShapeDtypeStruct((4, TOK), F32),
            jax.ShapeDtypeStruct((HID, 128), F32),
            jax.ShapeDtypeStruct((HID, 128), F32),
        ),
        in_specs=[vmem] * 6,
        out_specs=(vmem,) * 5,
        scratch_shapes=[
            V((2 * TOK, HALF), BF16), V((2 * TOK, HALF), BF16),
            V((4, 2 * TOK), jnp.int32), V((4, 2 * TOK), F32),
            V((ROWS, 2 * TOK), F32), V((NZ, 1, 2 * TOK), F32), V((NZ, 1, 2 * TOK), F32),
            V((ROWS, HALF), BF16), V((ROWS, HALF), BF16),
            V((2, ROWS, HALF), BF16), V((2, ROWS, HALF), BF16),
            V((2, ROWS, HID), BF16), V((2, ROWS, HID), BF16), V((ROWS, HID), F32),
            V((2, HID, HALF), BF16), V((2, HID, HALF), BF16),
            V((ROWS, HALF), BF16), V((ROWS, HALF), BF16),
            V((ROWS, HALF), BF16), V((ROWS, HALF), BF16),
            V((2 * TOK, ROWS), BF16), V((2 * TOK, ROWS), BF16), V((2 * TOK, ROWS), BF16),
            V((HID, ROWS), BF16), V((HID, ROWS), BF16),
            V((TOK, HALF), F32), V((TOK, HALF), BF16), V((TOK, HALF), BF16),
            V((TOK, HALF), F32), V((TOK, HALF), BF16), V((TOK, HALF), BF16),
            V((4, TOK), F32), V((4, TOK), F32), V((4, TOK), F32),
            V((4, TOK), F32), V((4, TOK), F32),
            V((2 * HID, 2 * HALF), BF16),
            V((2 * HID, 256), BF16), V((2 * HID, 256), BF16), V((2, 2 * HID, 256), BF16),
            V((2 * HID, 256), BF16), V((2 * HID, 256), BF16),
            V((2 * HID, 256), BF16), V((2 * HID, 256), BF16),
            V((2 * HID, 512), F32), V((2 * HID, 512), BF16),
            V((NYL, 2 * HID, 128), BF16),
            dma((PHASES, NZ)), dma((PHASES, NZ)), dma((7,)), dma((7,)),
            dma((YP_BACK + CHUNKS,)), dma((YP_BACK + CHUNKS,)),
            dma((6,)), dma((6,)), dma((NYL,)), dma((NYL,)),
        ],
        compiler_params=pltpu.CompilerParams(
            collective_id=0, has_side_effects=True, vmem_limit_bytes=60 * 1024 * 1024
        ),
    )(tokens, cotangent, routes.T, gates.T, w_in[0], w_out[0])
    mixed, grad_tokens, grad_gates, grad_in, grad_out = outs
    return mixed, grad_tokens, grad_gates.T, grad_in[None], grad_out[None]


def solution(mesh):
    placed = (
        P(("dp", "expert"), "tensor"),
        P(("dp", "expert"), None),
        P(("dp", "expert"), None),
        P("expert", "tensor", None),
        P("expert", "tensor", None),
        P(("dp", "expert"), "tensor"),
    )
    return jax.shard_map(
        per_device,
        mesh=mesh,
        in_specs=placed,
        out_specs=(
            P(("dp", "expert"), "tensor"),
            P(("dp", "expert"), "tensor"),
            P(("dp", "expert"), None),
            P("expert", "tensor", "dp"),
            P("expert", "tensor", "dp"),
        ),
        check_vma=False,
    )
```

```python
import functools

import jax
import jax.numpy as jnp
from jax import lax
from jax.experimental import pallas as pl
from jax.experimental.pallas import tpu as pltpu
from jax.sharding import PartitionSpec as P

MESH = pl.DeviceIdType.MESH
F32, BF16 = jnp.float32, jnp.bfloat16

NX, NYL = 4, 4
NZ, NYH = 8, 2
TOK = 128
CAP = 40
HEAD = 32
SLOTS = 2 * CAP
ROWS = NZ * SLOTS
HALF = 1024
HID = 384
PIECES = ((0, 512), (512, 256), (768, 128), (896, 128))
CHUNKS = len(PIECES)

PH_TOK_HEAD, PH_TOK_REST, PH_SC_HEAD, PH_SC_REST, PH_OUT, PH_BACK = range(6)
PHASES = PH_BACK + CHUNKS
SB_WIN, SB_WOUT, SB_HID, SB_PRE, SB_GATE = range(5)
YP_ROUTES, YP_GATES, YP_TOK, YP_COT, YP_MIX, YP_GG, YP_BACK = range(7)


def dot(a, b, dims):
    return lax.dot_general(a, b, (dims, ((), ())), preferred_element_type=F32)


NN = ((1,), (0,))
NT = ((1,), (1,))


def kernel(
    tok_in, cot_in, rt_in, gt_in, win_in, wout_in,
    mix_ref, gtok_ref, gg_ref, gin_ref, gout_ref,
    tok2, cot2, rt2, gt2, win_ref, wout_ref, sel, rankm, gatem,
    send_tok, send_sc, rows, scal, hid, pre, slope, wi, wo,
    out, back, rout, rback, g_hi, g_lo, sel_t, hid_t, pre_t,
    mixo, mixs, mixr, bko, bks, bkr, ggp, ggs, ggr, ggm, ggx,
    part, xa, xb, xs, x1, x2, xd1, xd2, xq, xqb, yr,
    zs, zr, ss, sr, hs, hr, ps, pr, xsm, xrm, ys, yrm, ls,
):
    dp = lax.axis_index("dp")
    ex = lax.axis_index("expert")
    c = lax.axis_index("tensor")
    x, yl = dp // NYL, dp % NYL
    z, yh = ex // NYH, ex % NYH
    sib = {"tensor": 1 - c}
    mirror = {"dp": x * NYL + (NYL - 1 - yl), "expert": z * NYH + (1 - yh)}
    x_up = {"dp": ((x + 1) % NX) * NYL + yl}
    x_dn = {"dp": ((x + NX - 1) % NX) * NYL + yl}

    def z_dev(other):
        return {"expert": other * NYH + yh}

    def y_dev(other):
        return {"dp": x * NYL + other}

    def rcopy(src, dst, send, recv, dev):
        return pltpu.make_async_remote_copy(
            src_ref=src, dst_ref=dst, send_sem=send, recv_sem=recv,
            device_id=dev, device_id_type=MESH,
        )

    barrier = pltpu.get_barrier_semaphore()

    def greet(dev):
        pl.semaphore_signal(barrier, inc=1, device_id=dev, device_id_type=MESH)

    for step in range(1, NZ):
        greet(z_dev((z + step) % NZ))
    for step in range(1, NYL):
        greet(y_dev((yl + step) % NYL))
    greet(sib)
    greet(mirror)
    greet(x_up)
    greet(x_dn)

    w_other = pl.ds(pl.multiple_of((1 - c) * HALF, 128), HALF)
    w_mine = pl.ds(pl.multiple_of(c * HALF, 128), HALF)
    own = pl.ds(0, TOK)
    local = [
        pltpu.make_async_copy(src, dst, ls.at[i])
        for i, (src, dst) in enumerate((
            (rt_in, rt2.at[:, own]),
            (gt_in, gt2.at[:, own]),
            (tok_in, tok2.at[own, :]),
            (cot_in, cot2.at[own, :]),
            (win_in, win_ref),
            (wout_in, wout_ref),
            (win_in.at[:, w_mine], wi.at[c]),
            (wout_in.at[:, w_mine], wo.at[c]),
        ))
    ]
    for cp in local:
        cp.start()
    local[0].wait()
    local[1].wait()
    before = (
        lax.broadcasted_iota(jnp.int32, (TOK, TOK), 0)
        < lax.broadcasted_iota(jnp.int32, (TOK, TOK), 1)
    ).astype(F32).astype(BF16)
    names = 2 * lax.broadcasted_iota(jnp.int32, (16, TOK), 0) + yh

    def place(block):
        cols = slice(block * TOK, (block + 1) * TOK)
        hits = jnp.zeros((16, TOK), F32)
        gate = jnp.zeros((16, TOK), F32)
        for k in range(4):
            hit = rt2[k : k + 1, cols] == names
            hits = hits + jnp.where(hit, 1.0, 0.0)
            gate = gate + jnp.where(hit, gt2[k : k + 1, cols], 0.0)
        rank = dot(hits.astype(BF16), before, NN)
        rank = jnp.where(hits > 0.0, rank, -5.0)
        for e in range(NZ):
            rankm[e, :, cols] = rank[e : e + 1]
            gatem[e, :, cols] = gate[e : e + 1]

    place(0)
    local[2].wait()
    head_slot = lax.broadcasted_iota(jnp.int32, (HEAD, TOK), 0).astype(F32)

    def own_head(e, carry):
        choose = jnp.where(rankm[e, :, 0:TOK] == head_slot, 1.0, 0.0).astype(BF16)
        at = pl.multiple_of(e * SLOTS, 16)
        send_tok[pl.ds(at, HEAD), :] = dot(choose, tok2[0:TOK, :], NN).astype(BF16)
        return carry

    lax.fori_loop(0, NZ, own_head, 0)

    pl.semaphore_wait(barrier, (NZ - 1) + (NYL - 1) + 4)

    y_in = [
        rcopy(rt2.at[:, own], rt2.at[:, pl.ds(TOK, TOK)], ps.at[YP_ROUTES], pr.at[YP_ROUTES], mirror),
        rcopy(gt2.at[:, own], gt2.at[:, pl.ds(TOK, TOK)], ps.at[YP_GATES], pr.at[YP_GATES], mirror),
        rcopy(tok2.at[own, :], tok2.at[pl.ds(TOK, TOK), :], ps.at[YP_TOK], pr.at[YP_TOK], mirror),
        rcopy(cot2.at[own, :], cot2.at[pl.ds(TOK, TOK), :], ps.at[YP_COT], pr.at[YP_COT], mirror),
    ]
    for cp in y_in[:3]:
        cp.start()
    local[3].wait()
    y_in[3].start()

    def z_copy(src, dst, lo, size, cols, phase, other, sender):
        s_at = pl.multiple_of(other * SLOTS + lo, 16)
        d_at = pl.multiple_of(sender * SLOTS + lo, 16)
        return rcopy(
            src.at[pl.ds(s_at, size), cols], dst.at[pl.ds(d_at, size), cols],
            zs.at[phase, other], zr.at[phase, sender], z_dev(other),
        )

    full = pl.ds(0, HALF)

    def z_send(src, dst, lo, size, cols, phase):
        def one(step, carry):
            z_copy(src, dst, lo, size, cols, phase, (z + step) % NZ, z).start()
            return carry

        lax.fori_loop(1, NZ, one, 0)

    def z_recv(src, dst, lo, size, cols, phase):
        def one(step, carry):
            other = (z + step) % NZ
            z_copy(src, dst, lo, size, cols, phase, other, other).wait_recv()
            return carry

        lax.fori_loop(1, NZ, one, 0)

    def z_sent(src, dst, lo, size, cols, phase):
        def one(step, carry):
            z_copy(src, dst, lo, size, cols, phase, (z + step) % NZ, z).wait_send()
            return carry

        lax.fori_loop(1, NZ, one, 0)

    here = pl.ds(pl.multiple_of(z * SLOTS, 16), SLOTS)
    rows_own, scal_own = rows.at[c], scal.at[c]
    z_send(send_tok, rows_own, 0, HEAD, full, PH_TOK_HEAD)

    w_cp = [
        rcopy(win_in.at[:, w_other], wi.at[c], ss.at[SB_WIN], sr.at[SB_WIN], sib),
        rcopy(wout_in.at[:, w_other], wo.at[c], ss.at[SB_WOUT], sr.at[SB_WOUT], sib),
    ]
    for cp in w_cp:
        cp.start()

    def scaled_head(e, carry):
        choose = jnp.where(rankm[e, :, 0:TOK] == head_slot, 1.0, 0.0)
        gate = jnp.sum(choose * gatem[e, :, 0:TOK], axis=1, keepdims=True)
        at = pl.multiple_of(e * SLOTS, 16)
        send_sc[pl.ds(at, HEAD), :] = (
            gate * dot(choose.astype(BF16), cot2[0:TOK, :], NN)
        ).astype(BF16)
        return carry

    lax.fori_loop(0, NZ, scaled_head, 0)
    z_send(send_sc, scal_own, 0, HEAD, full, PH_SC_HEAD)

    r_id = lax.broadcasted_iota(jnp.int32, (SLOTS, 2 * TOK), 0)
    t_id = lax.broadcasted_iota(jnp.int32, (SLOTS, 2 * TOK), 1)
    late = jnp.where(t_id >= TOK, 1, 0)
    second = jnp.where(
        r_id < 2 * HEAD,
        jnp.where(r_id >= HEAD, 1, 0),
        jnp.where(r_id >= HEAD + CAP, 1, 0),
    )
    slot = jnp.where(
        r_id < HEAD, r_id, jnp.where(r_id < HEAD + CAP, r_id - HEAD, r_id - CAP)
    )
    slot_map = jnp.where(second == late, slot, -1).astype(F32)

    y_in[0].wait_recv()
    y_in[1].wait_recv()
    place(1)
    y_in[2].wait_recv()

    def gather_tok(e, carry):
        choose = jnp.where(rankm[e] == slot_map, 1.0, 0.0)
        at = pl.multiple_of(e * SLOTS, 16)
        sel[pl.ds(at, SLOTS), :] = choose
        send_tok[pl.ds(at + HEAD, SLOTS - HEAD), :] = dot(
            choose[HEAD:].astype(BF16), tok2[...], NN
        ).astype(BF16)
        return carry

    lax.fori_loop(0, NZ, gather_tok, 0)
    z_send(send_tok, rows_own, HEAD, SLOTS - HEAD, full, PH_TOK_REST)
    rows[c, here, :] = send_tok[here, :]

    y_in[3].wait_recv()

    def gather_cot(e, carry):
        at = pl.ds(pl.multiple_of(e * SLOTS + HEAD, 16), SLOTS - HEAD)
        choose = sel[at, :]
        gate = jnp.sum(choose * gatem[e], axis=1, keepdims=True)
        send_sc[at, :] = (gate * dot(choose.astype(BF16), cot2[...], NN)).astype(BF16)
        return carry

    lax.fori_loop(0, NZ, gather_cot, 0)
    z_send(send_sc, scal_own, HEAD, SLOTS - HEAD, full, PH_SC_REST)
    scal[c, here, :] = send_sc[here, :]

    def gates_of(e, carry):
        at = pl.ds(pl.multiple_of(e * SLOTS, 16), SLOTS)
        out_gate = sel[at, :] * gatem[e]
        slope[at, 0 : 2 * TOK] = out_gate
        return carry

    lax.fori_loop(0, NZ, gates_of, 0)

    def turn(i, carry):
        at = pl.ds(pl.multiple_of(i * 128, 128), 128)
        g_t = slope[at, 0 : 2 * TOK].T
        hi = g_t.astype(BF16)
        g_hi[:, at] = hi
        g_lo[:, at] = (g_t - hi.astype(F32)).astype(BF16)
        sel_t[:, at] = sel[at, :].T.astype(BF16)
        return carry

    lax.fori_loop(0, ROWS // 128, turn, 0)

    def hand(buf, which, other):
        at = pl.ds(pl.multiple_of(other * SLOTS, 16), SLOTS)
        return rcopy(
            buf.at[c, at, :], buf.at[c, at, :], hs.at[which, other], hr.at[which, other], sib
        )

    def take(src, dst, buf, which, phase):
        def one(step, carry):
            other = (z + step) % NZ
            z_copy(src, dst, HEAD, SLOTS - HEAD, full, phase, other, other).wait_recv()
            hand(buf, which, other).start()
            return carry

        hand(buf, which, z).start()
        lax.fori_loop(1, NZ, one, 0)

        def ready(other, carry):
            hand(buf, which, other).wait_recv()
            return carry

        lax.fori_loop(0, NZ, ready, 0)

    def handed(buf, which):
        def one(other, carry):
            hand(buf, which, other).wait_send()
            return carry

        lax.fori_loop(0, NZ, one, 0)

    z_recv(send_tok, rows_own, 0, HEAD, full, PH_TOK_HEAD)
    take(send_tok, rows_own, rows, 0, PH_TOK_REST)
    for cp in local[4:]:
        cp.wait()

    TILE = 320

    def tile(i):
        return pl.ds(pl.multiple_of(i * TILE, 64), TILE)

    def forward(i, carry):
        at = tile(i)
        v = dot(rows[0, at, :], win_ref[:, 0:HALF], NT) + dot(
            rows[1, at, :], win_ref[:, HALF:], NT
        )
        s = 1.0 / (1.0 + jnp.exp(-v))
        hid[c, at, :] = (v * s).astype(BF16)
        slope[at, :] = s * (1.0 + v * (1.0 - s))
        return carry

    lax.fori_loop(0, ROWS // TILE, forward, 0)
    cp_hid = rcopy(hid.at[c], hid.at[c], ss.at[SB_HID], sr.at[SB_HID], sib)
    cp_hid.start()
    w_cp[0].wait_recv()
    w_cp[1].wait_recv()
    cp_hid.wait_recv()

    def project(i, carry):
        at = tile(i)
        out[at, :] = (dot(hid[0, at, :], wo[0], NN) + dot(hid[1, at, :], wo[1], NN)).astype(BF16)
        return carry

    lax.fori_loop(0, ROWS // TILE, project, 0)
    z_send(out, rout, 0, SLOTS, full, PH_OUT)
    rout[here, :] = out[here, :]

    def flip(src, dst):
        def one(i, carry):
            at = pl.ds(pl.multiple_of(i * 128, 128), 128)
            dst[:, at] = src[c, at, :].astype(F32).T.astype(BF16)
            return carry

        lax.fori_loop(0, ROWS // 128, one, 0)

    flip(hid, hid_t)

    z_recv(send_sc, scal_own, 0, HEAD, full, PH_SC_HEAD)
    take(send_sc, scal_own, scal, 1, PH_SC_REST)
    XW = 512
    XH = XW // 2
    up, dn, far = (x + 1) % NX, (x + NX - 1) % NX, (x + 2) % NX

    def weigh(which, lhs, rhs):
        for h in range(2):
            def one(n, carry, h=h):
                src = pl.ds(pl.multiple_of(n * 256, 256), 256)
                dst = pl.ds(pl.multiple_of(h * HALF + n * 256, 256), 256)
                part[which, :, dst] = dot(lhs[...], rhs[h, :, src], NN).astype(BF16)
                return carry

            lax.fori_loop(0, HALF // 256, one, 0)

    def x_cols(other, half):
        return pl.ds(pl.multiple_of(other * XW + half * XH, 256), XH)

    def x_cp(which, i, src, dst, dev):
        return rcopy(src, dst.at[which], xsm.at[which, i], xrm.at[which, i], dev)

    def x_copies(which):
        mine = part.at[which]
        return (
            x_cp(which, 0, mine.at[:, x_cols(far, 0)], xa, x_up),
            x_cp(which, 1, mine.at[:, x_cols(far, 1)], xb, x_dn),
            x_cp(which, 2, mine.at[:, x_cols(up, 1)], xd1, x_up),
            x_cp(which, 3, mine.at[:, x_cols(dn, 0)], xd2, x_dn),
            x_cp(which, 4, xs.at[which, 0], x1, x_up),
            x_cp(which, 5, xs.at[which, 1], x2, x_dn),
        )

    def x_add(which, cps):
        cps[0].wait_recv()
        xs[which, 0] = (
            part[which, :, x_cols(up, 0)].astype(F32) + xa[which].astype(F32)
        ).astype(BF16)
        cps[1].wait_recv()
        xs[which, 1] = (
            part[which, :, x_cols(dn, 1)].astype(F32) + xb[which].astype(F32)
        ).astype(BF16)
        cps[4].start()
        cps[5].start()

    def y_cols(other):
        return pl.ds(pl.multiple_of(other * 128, 128), 128)

    def y_copy(which, other, sender):
        return rcopy(
            xqb.at[which, :, y_cols(other)], yr.at[which, sender],
            ys.at[which, other], yrm.at[which, sender], y_dev(other),
        )

    def y_start(which, cps):
        for i in (2, 3, 4, 5):
            cps[i].wait_recv()
        mine = part.at[which]
        xq[which, :, 0:XH] = (
            mine[:, x_cols(x, 0)].astype(F32) + x1[which].astype(F32) + xd2[which].astype(F32)
        )
        xq[which, :, XH:] = (
            mine[:, x_cols(x, 1)].astype(F32) + x2[which].astype(F32) + xd1[which].astype(F32)
        )
        xqb[which] = xq[which].astype(BF16)
        for step in range(1, NYL):
            y_copy(which, (yl + step) % NYL, yl).start()

    def y_finish(which, ref):
        total = xq[which, :, y_cols(yl)]
        for step in range(1, NYL):
            other = (yl + step) % NYL
            y_copy(which, other, other).wait_recv()
            total = total + yr[which, other].astype(F32)
        ref[...] = total

    IN, OUT = 0, 1
    weigh(OUT, hid_t, scal)
    x_out = x_copies(OUT)
    for cp in x_out[:4]:
        cp.start()

    def backward(i, carry):
        at = tile(i)
        v = dot(scal[0, at, :], wout_ref[:, 0:HALF], NT) + dot(
            scal[1, at, :], wout_ref[:, HALF:], NT
        )
        pre[c, at, :] = (v * slope[at, :]).astype(BF16)
        return carry

    lax.fori_loop(0, ROWS // TILE, backward, 0)
    cp_pre = rcopy(pre.at[c], pre.at[c], ss.at[SB_PRE], sr.at[SB_PRE], sib)
    cp_pre.start()
    flip(pre, pre_t)
    weigh(IN, pre_t, rows)
    x_in = x_copies(IN)
    x_in[0].start()
    x_in[1].start()
    cp_pre.wait_recv()

    def project_back(i, carry):
        at = tile(i)
        back[at, :] = (dot(pre[0, at, :], wi[0], NN) + dot(pre[1, at, :], wi[1], NN)).astype(BF16)
        return carry

    lax.fori_loop(0, ROWS // TILE, project_back, 0)

    def piece(q):
        return pl.ds(*PIECES[q])

    for q in range(CHUNKS):
        z_send(back, rback, 0, SLOTS, piece(q), PH_BACK + q)
    rback[here, :] = back[here, :]
    x_add(OUT, x_out)
    x_in[2].start()
    x_in[3].start()
    x_add(IN, x_in)
    y_start(OUT, x_out)

    z_recv(out, rout, 0, SLOTS, full, PH_OUT)

    def mix(n, carry):
        at = pl.ds(pl.multiple_of(n * 256, 256), 256)
        m = dot(g_hi[...], rout[:, at], NN) + dot(g_lo[...], rout[:, at], NN)
        mixo[:, at] = m[0:TOK]
        mixs[:, at] = m[TOK:].astype(BF16)
        return carry

    lax.fori_loop(0, HALF // 256, mix, 0)
    cp_mix = rcopy(mixs, mixr, ps.at[YP_MIX], pr.at[YP_MIX], mirror)
    cp_mix.start()

    def inner(e, acc):
        at = pl.ds(pl.multiple_of(e * SLOTS, 16), SLOTS)
        dots = dot(rout[at, :], cot2[...], NT) * sel[at, :]
        per_token = jnp.sum(dots, axis=0, keepdims=True)
        hit = rt2[...] == 2 * e + yh
        return acc + jnp.where(hit, per_token, 0.0)

    gate_part = lax.fori_loop(0, NZ, inner, jnp.zeros((4, 2 * TOK), F32))
    ggp[...] = gate_part[:, 0:TOK]
    ggs[...] = gate_part[:, TOK:]
    cp_gg = rcopy(ggs, ggr, ps.at[YP_GG], pr.at[YP_GG], mirror)
    cp_gg.start()

    y_start(IN, x_in)

    cp_gg.wait_recv()
    ggm[...] = ggp[...] + ggr[...]
    cp_gs = rcopy(ggm, ggx, ss.at[SB_GATE], sr.at[SB_GATE], sib)
    cp_gs.start()
    cp_mix.wait_recv()
    mix_ref[...] = (mixo[...] + mixr[...].astype(F32)).astype(BF16)
    cp_gs.wait_recv()
    gg_ref[...] = ggm[...] + ggx[...]
    y_finish(OUT, gout_ref)
    y_finish(IN, gin_ref)

    cp_back = []
    for q in range(CHUNKS):
        z_recv(back, rback, 0, SLOTS, piece(q), PH_BACK + q)
        b = dot(sel_t[...], rback[:, piece(q)], NN)
        bko[:, piece(q)] = b[0:TOK]
        bks[:, piece(q)] = b[TOK:].astype(BF16)
        cp = rcopy(
            bks.at[:, piece(q)], bkr.at[:, piece(q)],
            ps.at[YP_BACK + q], pr.at[YP_BACK + q], mirror,
        )
        cp.start()
        cp_back.append(cp)
    for q in range(CHUNKS):
        cp_back[q].wait_recv()
        gtok_ref[:, piece(q)] = (bko[:, piece(q)] + bkr[:, piece(q)].astype(F32)).astype(BF16)

    z_sent(send_tok, rows_own, 0, HEAD, full, PH_TOK_HEAD)
    z_sent(send_tok, rows_own, HEAD, SLOTS - HEAD, full, PH_TOK_REST)
    z_sent(send_sc, scal_own, 0, HEAD, full, PH_SC_HEAD)
    z_sent(send_sc, scal_own, HEAD, SLOTS - HEAD, full, PH_SC_REST)
    z_sent(out, rout, 0, SLOTS, full, PH_OUT)
    for q in range(CHUNKS):
        z_sent(back, rback, 0, SLOTS, piece(q), PH_BACK + q)
    handed(rows, 0)
    handed(scal, 1)
    for which in range(2):
        for step in range(1, NYL):
            y_copy(which, (yl + step) % NYL, yl).wait_send()
    for cp in (*y_in, *w_cp, *x_out, *x_in, *cp_back, cp_hid, cp_pre, cp_mix, cp_gg, cp_gs):
        cp.wait_send()


def write(*refs):
    n = len(refs) // 2
    for src, dst in zip(refs[:n], refs[n:]):
        dst[...] = src[...]


def per_device(tokens, routes, gates, w_in, w_out, cotangent):
    vmem = pl.BlockSpec(memory_space=pltpu.VMEM)
    V = pltpu.VMEM
    dma = pltpu.SemaphoreType.DMA
    outs = pl.pallas_call(
        kernel,
        out_shape=(
            jax.ShapeDtypeStruct((TOK, HALF), BF16),
            jax.ShapeDtypeStruct((TOK, HALF), BF16),
            jax.ShapeDtypeStruct((4, TOK), F32),
            jax.ShapeDtypeStruct((HID, 128), F32),
            jax.ShapeDtypeStruct((HID, 128), F32),
        ),
        in_specs=[pl.BlockSpec(memory_space=pl.ANY)] * 6,
        out_specs=(vmem,) * 5,
        scratch_shapes=[
            V((2 * TOK, HALF), BF16), V((2 * TOK, HALF), BF16),
            V((4, 2 * TOK), jnp.int32), V((4, 2 * TOK), F32),
            V((HID, 2 * HALF), BF16), V((HID, 2 * HALF), BF16),
            V((ROWS, 2 * TOK), F32), V((NZ, 1, 2 * TOK), F32), V((NZ, 1, 2 * TOK), F32),
            V((ROWS, HALF), BF16), V((ROWS, HALF), BF16),
            V((2, ROWS, HALF), BF16), V((2, ROWS, HALF), BF16),
            V((2, ROWS, HID), BF16), V((2, ROWS, HID), BF16), V((ROWS, HID), F32),
            V((2, HID, HALF), BF16), V((2, HID, HALF), BF16),
            V((ROWS, HALF), BF16), V((ROWS, HALF), BF16),
            V((ROWS, HALF), BF16), V((ROWS, HALF), BF16),
            V((2 * TOK, ROWS), BF16), V((2 * TOK, ROWS), BF16), V((2 * TOK, ROWS), BF16),
            V((HID, ROWS), BF16), V((HID, ROWS), BF16),
            V((TOK, HALF), F32), V((TOK, HALF), BF16), V((TOK, HALF), BF16),
            V((TOK, HALF), F32), V((TOK, HALF), BF16), V((TOK, HALF), BF16),
            V((4, TOK), F32), V((4, TOK), F32), V((4, TOK), F32),
            V((4, TOK), F32), V((4, TOK), F32),
            V((2, HID, 2 * HALF), BF16),
            V((2, HID, 256), BF16), V((2, HID, 256), BF16), V((2, 2, HID, 256), BF16),
            V((2, HID, 256), BF16), V((2, HID, 256), BF16),
            V((2, HID, 256), BF16), V((2, HID, 256), BF16),
            V((2, HID, 512), F32), V((2, HID, 512), BF16),
            V((2, NYL, HID, 128), BF16),
            dma((PHASES, NZ)), dma((PHASES, NZ)), dma((5,)), dma((5,)),
            dma((2, NZ)), dma((2, NZ)),
            dma((YP_BACK + CHUNKS,)), dma((YP_BACK + CHUNKS,)),
            dma((2, 6)), dma((2, 6)), dma((2, NYL)), dma((2, NYL)), dma((8,)),
        ],
        compiler_params=pltpu.CompilerParams(
            collective_id=0, has_side_effects=True, vmem_limit_bytes=60 * 1024 * 1024
        ),
    )(tokens, cotangent, routes.T, gates.T, w_in[0], w_out[0])
    mixed, grad_tokens, grad_gates, grad_in, grad_out = pl.pallas_call(
        write,
        out_shape=tuple(jax.ShapeDtypeStruct(o.shape, o.dtype) for o in outs),
        in_specs=[vmem] * 5,
        out_specs=(vmem,) * 5,
    )(*outs)
    return mixed, grad_tokens, grad_gates.T, grad_in[None], grad_out[None]


def solution(mesh):
    placed = (
        P(("dp", "expert"), "tensor"),
        P(("dp", "expert"), None),
        P(("dp", "expert"), None),
        P("expert", "tensor", None),
        P("expert", "tensor", None),
        P(("dp", "expert"), "tensor"),
    )
    return jax.shard_map(
        per_device,
        mesh=mesh,
        in_specs=placed,
        out_specs=(
            P(("dp", "expert"), "tensor"),
            P(("dp", "expert"), "tensor"),
            P(("dp", "expert"), None),
            P("expert", "tensor", "dp"),
            P("expert", "tensor", "dp"),
        ),
        check_vma=False,
    )
```
